32 devices in a mesh: groups: 2 (over y), head: 4 (over z), hist: 4 (over x, core).
Axes of the slice: x: 2, y: 2, z: 4, core: 2. Of those that a mesh axis runs over, the one named last changes fastest.
Arguments:
- tokens: bfloat16 [1024, 8192], P('groups', 'hist'), parts along dimension 0, may hold values from -6 to 6
- w_qkvu: bfloat16 [8192, 4, 8192], P('hist', None, 'head'), may hold values from -0.0625 to 0.0625
- k_cache: bfloat16 [4096, 8192], P(('groups', 'hist'), 'head'), parts along dimension 0, may hold values from -6 to 6
- v_cache: bfloat16 [4096, 8192], P(('groups', 'hist'), 'head'), parts along dimension 0
- w_out: bfloat16 [8192, 8192], P('head', 'hist'), may hold values from -0.0625 to 0.0625
- vis_start: int32 [1024], P('groups'), parts along dimension 0, may hold values from 0 to 511, as said below
- vis_end: int32 [1024], P('groups'), parts along dimension 0, may hold values from 1025 to 2048
Outputs:
- layer_out: bfloat16 [1024, 8192], P(('groups', 'head'), 'hist'), parts along dimension 0
The draws below stay inside these ranges and needn't reach their ends.
There are 2 independent parts, one for each index of `groups`. The reference program is written for one: setup_inputs(seed, part) draws one part's arguments, and reference() takes and returns one part's arrays. A program takes and returns all parts, laid end to end along the dimension named above; an argument that names none is the same for every part. Nothing has to cross between parts.
Inputs may be any that keep to these rules, and one draw needn't show every extreme that they name: vis_start and vis_end together leave every candidate 2048 // 4 + 2 or more visible history events.
All inputs are finite; a program needn't handle non-finite values.
Results may differ from the reference program's by a relative error of at most 0.02.
Values may be sent and summed in bfloat16 or wider, within the bound.
A program may use at most 192 MiB of HBM per device.

```python
import jax
import jax.numpy as jnp
from jax import lax

D = 8192
HEADS = 64
DH = 128
HD = 8192
HIST = 2048
CAND = 512
N_HIST = 4


def spread_ends(base_key, low_draw, high_draw, low_end, high_end):
    pick_key, value_key = jax.random.split(base_key)
    drawn = jax.random.randint(value_key, (CAND,), low_draw, high_draw)
    shuffled = jax.random.permutation(pick_key, CAND)
    places = lax.iota(jnp.int32, CAND)
    drawn = jnp.where(places == shuffled[0], low_end, drawn)
    drawn = jnp.where(places == shuffled[1], high_end, drawn)
    return drawn.astype(jnp.int32)


def draw_vis_start(key, part):
    return spread_ends(jax.random.fold_in(key, 11), 0, HIST // 4, 0, HIST // 4 - 1)


def draw_vis_end(key, part):
    return spread_ends(jax.random.fold_in(key, 23), HIST // 2 + 1, HIST + 1, HIST // 2 + 1, HIST)


def draw_v_cache(key, part):
    base_key, scale_key = jax.random.split(jax.random.fold_in(key, 37), 2)
    columns = lax.iota(jnp.float32, HD) / HD
    column_scale = 0.5 * 10.0 ** columns * jax.random.uniform(scale_key, (HD,), minval=0.7, maxval=1.4)
    entries = jax.random.normal(base_key, (HIST, HD))
    return (entries * column_scale[None, :]).astype(jnp.bfloat16)


def level_of(rng, shape, shards, smallest, top_value):
    level, own = 1.0, jax.random.fold_in(rng, 6)
    for position, blocks in shards:
        draws = jnp.exp(jax.random.uniform(jax.random.fold_in(own, position), (blocks,), jnp.float32, smallest / len(shards), top_value / len(shards)))
        level = level * jnp.repeat(draws, shape[position] // blocks).reshape([-1 if axis == position else 1 for axis in range(len(shape))])
    return level


def normal_values(rng, extent, spread, most, pieces=(), dtype=jnp.bfloat16):
    result = spread * jax.random.normal(rng, extent, jnp.float32)
    if pieces:
        result = result * level_of(rng, extent, pieces, -0.22, 0.18)
    return jnp.clip(result, -most, most).astype(dtype)


def setup_inputs(seed: int = 0, part: int = 0) -> dict:
    splits = jax.random.split(jax.random.key(seed), 8)
    own_keys = jax.random.split(jax.random.fold_in(splits[7], part), 8)
    tokens = normal_values(own_keys[0], (CAND, D), 1.0, 6.0, ((1, 4),))
    w_qkvu = normal_values(splits[1], (D, 4, HD), D ** -0.5, 0.0625, ((0, 4), (2, 4)))
    k_cache = normal_values(own_keys[2], (HIST, HD), 1.0, 6.0, ((0, 4), (1, 4)))
    v_cache = draw_v_cache(jax.random.fold_in(jax.random.fold_in(splits[7], part), 71), part)
    w_out = normal_values(splits[4], (HD, D), HD ** -0.5, 0.0625, ((0, 4), (1, 4)))
    vis_start = draw_vis_start(jax.random.fold_in(jax.random.fold_in(splits[7], part), 71), part)
    vis_end = draw_vis_end(jax.random.fold_in(jax.random.fold_in(splits[7], part), 71), part)
    return dict(tokens=tokens, w_qkvu=w_qkvu, k_cache=k_cache, v_cache=v_cache, w_out=w_out, vis_start=vis_start, vis_end=vis_end)


epsilon = 1e-05

def project_all(tokens, w_qkvu):
    row_block = D // N_HIST
    flat_weight = w_qkvu.reshape(D, 4 * HD)
    running_sum = jnp.zeros((CAND, 4 * HD), jnp.float32)
    for block_index in range(N_HIST):
        lower_row = block_index * row_block
        partial_term = jnp.dot(tokens[:, lower_row:lower_row + row_block], flat_weight[lower_row:lower_row + row_block], preferred_element_type=jnp.float32)
        rounded = lax.optimization_barrier(partial_term.astype(jnp.bfloat16))
        running_sum = running_sum + rounded.astype(jnp.float32)
    return jax.nn.silu(running_sum).astype(jnp.bfloat16).reshape(CAND, 4, HD)

def reference(tokens, w_qkvu, k_cache, v_cache, w_out, vis_start, vis_end):
    projected = project_all(tokens, w_qkvu)
    queries = projected[:, 0].reshape(CAND, HEADS, DH).transpose(1, 0, 2)
    self_keys = projected[:, 1].reshape(CAND, HEADS, DH).transpose(1, 0, 2)
    self_values = projected[:, 2].reshape(CAND, HEADS, DH).transpose(1, 0, 2)
    gate_part = projected[:, 3]
    key_heads = k_cache.reshape(HIST, HEADS, DH).transpose(1, 0, 2)
    value_heads = v_cache.reshape(HIST, HEADS, DH).transpose(1, 0, 2)
    positions = lax.iota(jnp.int32, HIST)
    visible = (positions[None, :] >= vis_start[:, None]) & (positions[None, :] < vis_end[:, None])
    counts = (vis_end - vis_start).astype(jnp.float32)

    def head_output(operands):
        head_query, self_key, self_value, key_head, value_head = operands
        scores = jnp.dot(head_query, key_head.T, preferred_element_type=jnp.float32) * DH ** (-0.5)
        weights = jnp.where(visible, jax.nn.silu(scores), 0.0).astype(jnp.bfloat16)
        history = jnp.dot(weights, value_head, preferred_element_type=jnp.float32)
        own_score = lax.optimization_barrier(jnp.sum(head_query.astype(jnp.float32) * self_key.astype(jnp.float32), axis=1)) * DH ** (-0.5)
        return history / jnp.sqrt(counts)[:, None] + jax.nn.silu(own_score)[:, None] * self_value.astype(jnp.float32)
    per_head = lax.map(head_output, (queries, self_keys, self_values, key_heads, value_heads))
    attended = per_head.transpose(1, 0, 2).reshape(CAND, HD)
    mean_value = lax.optimization_barrier(jnp.sum(attended, axis=1)) / HD
    centered = attended - mean_value[:, None]
    variance = lax.optimization_barrier(jnp.sum(centered * centered, axis=1)) / HD
    normed = centered * lax.rsqrt(variance + epsilon)[:, None]
    gated = (normed * gate_part.astype(jnp.float32)).astype(jnp.bfloat16)
    projected_out = jnp.dot(gated, w_out, preferred_element_type=jnp.float32)
    return (tokens.astype(jnp.float32) + projected_out).astype(jnp.bfloat16)
```

```python
import functools

import jax
import jax.numpy as jnp
from jax import lax
from jax.experimental import pallas as pl
from jax.experimental.pallas import tpu as pltpu
from jax.sharding import PartitionSpec as P

DH = 128
TILE = 256


epsilon = 1e-05


def history_terms(query_heads, key_block, value_block, vis_lo, vis_hi):
    head_total = query_heads.shape[1]
    head_size = query_heads.shape[2]
    block_len = key_block.shape[0]
    key_heads = key_block.reshape(block_len, head_total, head_size)
    value_heads = value_block.reshape(block_len, head_total, head_size)
    scores = jnp.einsum(
        "rhe,lhe->rhl", query_heads, key_heads, preferred_element_type=jnp.float32
    ) * head_size ** (-0.5)
    positions = lax.iota(jnp.int32, block_len)
    visible = (positions[None, :] >= vis_lo[:, None]) & (positions[None, :] < vis_hi[:, None])
    weights = jnp.where(visible[:, None, :], jax.nn.silu(scores), 0.0).astype(jnp.bfloat16)
    summed_values = jnp.einsum(
        "rhl,lhe->rhe", weights, value_heads, preferred_element_type=jnp.float32
    )
    return summed_values.reshape(query_heads.shape[0], head_total * head_size)


def local(tokens, w_qkvu, k_cache, v_cache, w_out, vis_start, vis_end):
    cand_total = tokens.shape[0]
    hist_count = lax.axis_size("hist")
    head_count = lax.axis_size("head")
    own_count = cand_total // hist_count
    own_first = lax.axis_index("hist") * own_count
    local_width = w_qkvu.shape[2]
    local_heads = local_width // DH
    full_width = local_width * head_count
    flat_weight = w_qkvu.reshape(w_qkvu.shape[0], 4 * local_width)
    start_own = lax.dynamic_slice_in_dim(vis_start, own_first, own_count)
    end_own = lax.dynamic_slice_in_dim(vis_end, own_first, own_count)
    summed = lax.psum_scatter(
        jnp.dot(tokens, flat_weight, preferred_element_type=jnp.float32).astype(jnp.bfloat16),
        "hist",
        scatter_dimension=0,
        tiled=True,
    ).astype(jnp.float32)
    own_part = jax.nn.silu(summed).astype(jnp.bfloat16).reshape(own_count, 4, local_width)
    own_query = own_part[:, 0]
    own_key = own_part[:, 1]
    own_value = own_part[:, 2]
    own_gate = own_part[:, 3]
    query_heads = own_query.reshape(own_count, local_heads, DH)
    history = history_terms(
        query_heads,
        lax.all_gather(k_cache, "hist", axis=0, tiled=True),
        lax.all_gather(v_cache, "hist", axis=0, tiled=True),
        start_own,
        end_own,
    )
    counts = (end_own - start_own).astype(jnp.float32)
    own_product = own_query.astype(jnp.float32) * own_key.astype(jnp.float32)
    own_score = jnp.sum(own_product.reshape(own_count, local_heads, DH), axis=2) * DH ** (-0.5)
    own_term = jax.nn.silu(own_score)[:, :, None] * own_value.astype(jnp.float32).reshape(
        own_count, local_heads, DH
    )
    attended = history / jnp.sqrt(counts)[:, None] + own_term.reshape(own_count, local_width)
    row_sum = lax.psum(jnp.sum(attended, axis=1), "head")
    centered = attended - (row_sum / full_width)[:, None]
    spread = lax.psum(jnp.sum(centered * centered, axis=1), "head")
    normed = centered * lax.rsqrt(spread / full_width + epsilon)[:, None]
    gated_rows = (normed * own_gate.astype(jnp.float32)).astype(jnp.bfloat16)
    gathered = lax.all_gather(gated_rows, "hist", axis=0, tiled=True)
    out_count = cand_total // head_count
    out_first = lax.axis_index("head") * out_count
    whole_out = jnp.dot(gathered, w_out, preferred_element_type=jnp.float32)
    total_out = lax.psum(whole_out.astype(jnp.bfloat16), "head").astype(jnp.float32)
    summed_out = lax.dynamic_slice_in_dim(total_out, out_first, out_count, 0)
    residual = lax.dynamic_slice_in_dim(tokens, out_first, out_count, 0).astype(jnp.float32)
    return (residual + summed_out).astype(jnp.bfloat16)


def silu(v):
    h = 0.5 * v
    return h + h * jnp.tanh(h)


def history_kernel(
    n_tiles, tok_ref, w_ref, k_ref, v_ref, lo_ref, hi_ref, att_ref, gate_ref,
    acc, mask, mine, s1, r1, s2q, r2q, s2k, r2k, s3, r3, kv, s4, r4, part, s5, r5, ssem, rsem,
):
    step = pl.program_id(0)
    me = lax.axis_index("hist")
    x = me // 2
    c = me % 2
    partner = 2 * x + (1 - c)
    across = 2 * (1 - x) + c
    rows = tok_ref.shape[0] // 4
    depth = tok_ref.shape[1]
    tile = w_ref.shape[2]
    events = k_ref.shape[0]

    def quarter(xx, cc):
        return pl.ds(pl.multiple_of((2 * xx + cc) * rows, rows), rows)

    def columns(t, size, base=0):
        return pl.ds(pl.multiple_of(t * tile + base, 128), size)

    def copy(kind, src, dst, t, target):
        return pltpu.make_async_remote_copy(
            src_ref=src.at[t], dst_ref=dst.at[t],
            send_sem=ssem.at[kind, t], recv_sem=rsem.at[kind, t],
            device_id={"hist": target}, device_id_type=pl.DeviceIdType.MESH,
        )

    def copy1(t):
        return copy(0, s1, r1, t, partner)

    def copy2q(t):
        return copy(1, s2q, r2q, t, across)

    def copy2k(t):
        return copy(2, s2k, r2k, t, across)

    def copy3(t):
        return copy(3, s3, r3, t, partner)

    def copy4(t):
        return copy(4, s4, r4, t, partner)

    def copy5(t):
        return copy(5, s5, r5, t, across)

    @pl.when(step == 0)
    def _():
        barrier = pltpu.get_barrier_semaphore()
        for other in (partner, across):
            pl.semaphore_signal(
                barrier, inc=1, device_id={"hist": other}, device_id_type=pl.DeviceIdType.MESH
            )
        pl.semaphore_wait(barrier, 2)
        for half in range(2):
            for xx in range(2):
                q = quarter(xx, c if half == 0 else 1 - c)
                lo = lo_ref[q, :]
                hi = hi_ref[q, :]
                for e in range(events // 128):
                    pos = me * events + e * 128 + lax.broadcasted_iota(jnp.int32, lo.shape, 1)
                    seen = (pos >= lo) & (pos < hi)
                    mask[half, xx * rows:(xx + 1) * rows, e * 128:(e + 1) * 128] = jnp.where(
                        seen, 1.0, 0.0
                    )

    @pl.when((step >= 5) & (step < n_tiles + 5))
    def _():
        t = step - 5
        copy5(t).wait()
        lo = lo_ref[quarter(x, c), :]
        hi = hi_ref[quarter(x, c), :]
        inv = lax.rsqrt((hi - lo).astype(jnp.float32))
        for h in range(tile // DH):
            cols = slice(h * DH, (h + 1) * DH)
            hist = part[t, x, :, cols] + r5[t, :, cols].astype(jnp.float32)
            q = s3[t, x, :, cols].astype(jnp.float32)
            kk = kv[t, :, cols].astype(jnp.float32)
            vv = kv[t, :, tile + h * DH:tile + (h + 1) * DH].astype(jnp.float32)
            score = jnp.sum(q * kk, axis=1, keepdims=True) * DH ** (-0.5)
            att_ref[:, columns(t, DH, h * DH)] = hist * inv + silu(score) * vv

    @pl.when((step >= 4) & (step < n_tiles + 4))
    def _():
        t = step - 4
        copy4(t).wait()
        s5[t] = (part[t, 1 - x] + r4[t, 1 - x].astype(jnp.float32)).astype(jnp.bfloat16)
        copy5(t).start()
        part[t, x] = part[t, x] + r4[t, x].astype(jnp.float32)

    @pl.when((step >= 2) & (step < n_tiles + 2))
    def _():
        t = step - 2
        copy2q(t).wait()
        s3[t] = silu(s2q[t].astype(jnp.float32) + r2q[t].astype(jnp.float32)).astype(jnp.bfloat16)
        copy3(t).start()
        copy2k(t).wait()
        own = silu(mine[t, x, :, tile:].astype(jnp.float32) + r2k[t].astype(jnp.float32))
        own = own.astype(jnp.bfloat16)
        kv[t] = own[:, :2 * tile]
        gate_ref[:, columns(t, tile)] = own[:, 2 * tile:]

    @pl.when((step >= 1) & (step < n_tiles + 1))
    def _():
        t = step - 1
        copy1(t).wait()
        for xx in range(2):
            both = mine[t, xx, :, :tile].astype(jnp.float32) + r1[t, xx, :, :tile].astype(jnp.float32)
            s2q[t, xx] = both.astype(jnp.bfloat16)
        copy2q(t).start()
        both = mine[t, 1 - x, :, tile:].astype(jnp.float32) + r1[t, 1 - x, :, tile:].astype(jnp.float32)
        s2k[t] = both.astype(jnp.bfloat16)
        copy2k(t).start()
        both = mine[t, x, :, tile:].astype(jnp.float32) + r1[t, x, :, tile:].astype(jnp.float32)
        mine[t, x, :, tile:] = both.astype(jnp.bfloat16)

    @pl.when((step >= 3) & (step < n_tiles + 3))
    def _():
        t = step - 3
        copy3(t).wait()
        for half in (1, 0):
            src = s3 if half == 0 else r3
            for h in range(tile // DH):
                cols = slice(h * DH, (h + 1) * DH)
                q = src[t, :, :, cols].reshape(2 * rows, DH)
                scores = lax.dot_general(
                    q, k_ref[:, columns(t, DH, h * DH)], (((1,), (1,)), ((), ())),
                    preferred_element_type=jnp.float32,
                )
                weights = (silu(scores * DH ** (-0.5)) * mask[half]).astype(jnp.bfloat16)
                out = jnp.dot(
                    weights, v_ref[:, columns(t, DH, h * DH)], preferred_element_type=jnp.float32
                ).reshape(2, rows, DH)
                if half == 0:
                    part[t, :, :, cols] = out
                else:
                    s4[t, :, :, cols] = out.astype(jnp.bfloat16)
            if half == 1:
                copy4(t).start()

    @pl.when(step < n_tiles)
    def _():
        t = step
        chunk = min(512, depth)
        for d in range(depth // chunk):
            block = w_ref[d * chunk:(d + 1) * chunk]
            flat = jnp.concatenate([block[:, j, :] for j in range(4)], axis=1)
            term = jnp.dot(
                tok_ref[:, d * chunk:(d + 1) * chunk], flat, preferred_element_type=jnp.float32
            )
            if d == 0:
                acc[...] = term
            else:
                acc[...] += term
        for xx in range(2):
            s1[t, xx] = acc[quarter(xx, 1 - c), :].astype(jnp.bfloat16)
        copy1(t).start()
        for xx in range(2):
            mine[t, xx] = acc[quarter(xx, c), :].astype(jnp.bfloat16)


def fused_history(tokens, w_qkvu, k_cache, v_cache, vis_start, vis_end):
    cand, depth = tokens.shape
    width = w_qkvu.shape[2]
    events = k_cache.shape[0]
    n_tiles = width // TILE
    rows = cand // 4
    lo = jnp.broadcast_to(vis_start[:, None], (cand, 128))
    hi = jnp.broadcast_to(vis_end[:, None], (cand, 128))

    def whole(shape):
        return pl.BlockSpec(shape, lambda i: (0, 0), pipeline_mode=pl.Buffered(1))

    def half(extra, cols):
        return pltpu.VMEM((n_tiles,) + extra + (rows, cols), jnp.bfloat16)

    return pl.pallas_call(
        functools.partial(history_kernel, n_tiles),
        grid=(n_tiles + 5,),
        in_specs=[
            whole((cand, depth)),
            pl.BlockSpec((depth, 4, TILE), lambda i: (0, 0, jnp.minimum(i, n_tiles - 1))),
            whole((events, width)),
            whole((events, width)),
            whole((cand, 128)),
            whole((cand, 128)),
        ],
        out_specs=[whole((rows, width)), whole((rows, width))],
        out_shape=[
            jax.ShapeDtypeStruct((rows, width), jnp.float32),
            jax.ShapeDtypeStruct((rows, width), jnp.bfloat16),
        ],
        scratch_shapes=[
            pltpu.VMEM((cand, 4 * TILE), jnp.float32),
            pltpu.VMEM((2, 2 * rows, events), jnp.float32),
            half((2,), 4 * TILE),
            half((2,), 4 * TILE), half((2,), 4 * TILE),
            half((2,), TILE), half((2,), TILE),
            half((), 3 * TILE), half((), 3 * TILE),
            half((2,), TILE), half((2,), TILE),
            half((), 2 * TILE),
            half((2,), TILE), half((2,), TILE),
            pltpu.VMEM((n_tiles, 2, rows, TILE), jnp.float32),
            half((), TILE), half((), TILE),
            pltpu.SemaphoreType.DMA((6, n_tiles)),
            pltpu.SemaphoreType.DMA((6, n_tiles)),
        ],
        compiler_params=pltpu.CompilerParams(
            vmem_limit_bytes=62 << 20, collective_id=0, has_side_effects=True
        ),
        name="history",
    )(tokens, w_qkvu, k_cache, v_cache, lo, hi)


def local_fused(tokens, w_qkvu, k_cache, v_cache, w_out, vis_start, vis_end):
    cand_total = tokens.shape[0]
    head_count = lax.axis_size("head")
    local_width = w_qkvu.shape[2]
    full_width = local_width * head_count
    attended, gate = fused_history(tokens, w_qkvu, k_cache, v_cache, vis_start, vis_end)
    local_mean = jnp.mean(attended, axis=1)
    off = attended - local_mean[:, None]
    local_sq = jnp.sum(off * off, axis=1)
    both = lax.all_gather(jnp.stack([local_mean, local_sq]), "head", axis=0)
    mean = jnp.mean(both[:, 0], axis=0)
    shift = both[:, 0] - mean[None]
    spread = jnp.sum(both[:, 1] + local_width * shift * shift, axis=0)
    normed = (attended - mean[:, None]) * lax.rsqrt(spread / full_width + epsilon)[:, None]
    gated_rows = (normed * gate.astype(jnp.float32)).astype(jnp.bfloat16)
    gathered = lax.all_gather(gated_rows, "hist", axis=0, tiled=True)
    out_count = cand_total // head_count
    out_first = lax.axis_index("head") * out_count
    whole_out = jnp.dot(gathered, w_out, preferred_element_type=jnp.float32)
    summed_out = lax.psum_scatter(
        whole_out.astype(jnp.bfloat16), "head", scatter_dimension=0, tiled=True
    ).astype(jnp.float32)
    residual = lax.dynamic_slice_in_dim(tokens, out_first, out_count, 0).astype(jnp.float32)
    return (residual + summed_out).astype(jnp.bfloat16)


def solution(mesh):
    in_specs = (
        P("groups", "hist"),
        P("hist", None, "head"),
        P(("groups", "hist"), "head"),
        P(("groups", "hist"), "head"),
        P("head", "hist"),
        P("groups"),
        P("groups"),
    )
    out_specs = P(("groups", "head"), "hist")
    body = local_fused if mesh.shape["hist"] == 4 else local
    return jax.shard_map(body, mesh=mesh, in_specs=in_specs, out_specs=out_specs, check_vma=False)
```

```python
import functools

import jax
import jax.numpy as jnp
from jax import lax
from jax.experimental import pallas as pl
from jax.experimental.pallas import tpu as pltpu
from jax.sharding import PartitionSpec as P

DH = 128
TILE = 256


epsilon = 1e-05


def history_terms(query_heads, key_block, value_block, vis_lo, vis_hi):
    head_total = query_heads.shape[1]
    head_size = query_heads.shape[2]
    block_len = key_block.shape[0]
    key_heads = key_block.reshape(block_len, head_total, head_size)
    value_heads = value_block.reshape(block_len, head_total, head_size)
    scores = jnp.einsum(
        "rhe,lhe->rhl", query_heads, key_heads, preferred_element_type=jnp.float32
    ) * head_size ** (-0.5)
    positions = lax.iota(jnp.int32, block_len)
    visible = (positions[None, :] >= vis_lo[:, None]) & (positions[None, :] < vis_hi[:, None])
    weights = jnp.where(visible[:, None, :], jax.nn.silu(scores), 0.0).astype(jnp.bfloat16)
    summed_values = jnp.einsum(
        "rhl,lhe->rhe", weights, value_heads, preferred_element_type=jnp.float32
    )
    return summed_values.reshape(query_heads.shape[0], head_total * head_size)


def local(tokens, w_qkvu, k_cache, v_cache, w_out, vis_start, vis_end):
    cand_total = tokens.shape[0]
    hist_count = lax.axis_size("hist")
    head_count = lax.axis_size("head")
    own_count = cand_total // hist_count
    own_first = lax.axis_index("hist") * own_count
    local_width = w_qkvu.shape[2]
    local_heads = local_width // DH
    full_width = local_width * head_count
    flat_weight = w_qkvu.reshape(w_qkvu.shape[0], 4 * local_width)
    start_own = lax.dynamic_slice_in_dim(vis_start, own_first, own_count)
    end_own = lax.dynamic_slice_in_dim(vis_end, own_first, own_count)
    summed = lax.psum_scatter(
        jnp.dot(tokens, flat_weight, preferred_element_type=jnp.float32).astype(jnp.bfloat16),
        "hist",
        scatter_dimension=0,
        tiled=True,
    ).astype(jnp.float32)
    own_part = jax.nn.silu(summed).astype(jnp.bfloat16).reshape(own_count, 4, local_width)
    own_query = own_part[:, 0]
    own_key = own_part[:, 1]
    own_value = own_part[:, 2]
    own_gate = own_part[:, 3]
    query_heads = own_query.reshape(own_count, local_heads, DH)
    history = history_terms(
        query_heads,
        lax.all_gather(k_cache, "hist", axis=0, tiled=True),
        lax.all_gather(v_cache, "hist", axis=0, tiled=True),
        start_own,
        end_own,
    )
    counts = (end_own - start_own).astype(jnp.float32)
    own_product = own_query.astype(jnp.float32) * own_key.astype(jnp.float32)
    own_score = jnp.sum(own_product.reshape(own_count, local_heads, DH), axis=2) * DH ** (-0.5)
    own_term = jax.nn.silu(own_score)[:, :, None] * own_value.astype(jnp.float32).reshape(
        own_count, local_heads, DH
    )
    attended = history / jnp.sqrt(counts)[:, None] + own_term.reshape(own_count, local_width)
    row_sum = lax.psum(jnp.sum(attended, axis=1), "head")
    centered = attended - (row_sum / full_width)[:, None]
    spread = lax.psum(jnp.sum(centered * centered, axis=1), "head")
    normed = centered * lax.rsqrt(spread / full_width + epsilon)[:, None]
    gated_rows = (normed * own_gate.astype(jnp.float32)).astype(jnp.bfloat16)
    gathered = lax.all_gather(gated_rows, "hist", axis=0, tiled=True)
    out_count = cand_total // head_count
    out_first = lax.axis_index("head") * out_count
    whole_out = jnp.dot(gathered, w_out, preferred_element_type=jnp.float32)
    total_out = lax.psum(whole_out.astype(jnp.bfloat16), "head").astype(jnp.float32)
    summed_out = lax.dynamic_slice_in_dim(total_out, out_first, out_count, 0)
    residual = lax.dynamic_slice_in_dim(tokens, out_first, out_count, 0).astype(jnp.float32)
    return (residual + summed_out).astype(jnp.bfloat16)


def silu(v):
    h = 0.5 * v
    return h + h * jnp.tanh(h)


def history_kernel(
    n_tiles, tok_ref, w_ref, k_ref, v_ref, lo_ref, hi_ref, att_ref, gate_ref,
    acc, mask, mine, s1, r1, s2q, r2q, s2k, r2k, s3, r3, kv, s4, r4, part, s5, r5, ssem, rsem,
):
    step = pl.program_id(0)
    me = lax.axis_index("hist")
    x = me // 2
    c = me % 2
    partner = 2 * x + (1 - c)
    across = 2 * (1 - x) + c
    rows = tok_ref.shape[0] // 4
    depth = tok_ref.shape[1]
    tile = w_ref.shape[2]
    events = k_ref.shape[0]

    def quarter(xx, cc):
        return pl.ds(pl.multiple_of((2 * xx + cc) * rows, rows), rows)

    def columns(t, size, base=0):
        return pl.ds(pl.multiple_of(t * tile + base, 128), size)

    def copy(kind, src, dst, t, target):
        return pltpu.make_async_remote_copy(
            src_ref=src.at[t], dst_ref=dst.at[t],
            send_sem=ssem.at[kind, t], recv_sem=rsem.at[kind, t],
            device_id={"hist": target}, device_id_type=pl.DeviceIdType.MESH,
        )

    def copy1(t):
        return copy(0, s1, r1, t, partner)

    def copy2q(t):
        return copy(1, s2q, r2q, t, across)

    def copy2k(t):
        return copy(2, s2k, r2k, t, across)

    def copy3(t):
        return copy(3, s3, r3, t, partner)

    def copy4(t):
        return copy(4, s4, r4, t, partner)

    def copy5(t):
        return copy(5, s5, r5, t, across)

    @pl.when(step == 0)
    def _():
        barrier = pltpu.get_barrier_semaphore()
        for other in (partner, across):
            pl.semaphore_signal(
                barrier, inc=1, device_id={"hist": other}, device_id_type=pl.DeviceIdType.MESH
            )
        pl.semaphore_wait(barrier, 2)
        for half in range(2):
            for xx in range(2):
                q = quarter(xx, c if half == 0 else 1 - c)
                lo = lo_ref[q, :]
                hi = hi_ref[q, :]
                for e in range(events // 128):
                    pos = me * events + e * 128 + lax.broadcasted_iota(jnp.int32, lo.shape, 1)
                    seen = (pos >= lo) & (pos < hi)
                    mask[half, xx * rows:(xx + 1) * rows, e * 128:(e + 1) * 128] = jnp.where(
                        seen, 1.0, 0.0
                    )

    @pl.when((step >= 5) & (step < n_tiles + 5))
    def _():
        t = step - 5
        copy5(t).wait()
        lo = lo_ref[quarter(x, c), :]
        hi = hi_ref[quarter(x, c), :]
        inv = lax.rsqrt((hi - lo).astype(jnp.float32))
        for h in range(tile // DH):
            cols = slice(h * DH, (h + 1) * DH)
            hist = part[t, x, :, cols] + r5[t, :, cols].astype(jnp.float32)
            q = s3[t, x, :, cols].astype(jnp.float32)
            kk = kv[t, :, cols].astype(jnp.float32)
            vv = kv[t, :, tile + h * DH:tile + (h + 1) * DH].astype(jnp.float32)
            score = jnp.sum(q * kk, axis=1, keepdims=True) * DH ** (-0.5)
            att_ref[:, columns(t, DH, h * DH)] = hist * inv + silu(score) * vv

    @pl.when((step >= 4) & (step < n_tiles + 4))
    def _():
        t = step - 4
        copy4(t).wait()
        s5[t] = (part[t, 1 - x] + r4[t, 1 - x].astype(jnp.float32)).astype(jnp.bfloat16)
        copy5(t).start()
        part[t, x] = part[t, x] + r4[t, x].astype(jnp.float32)

    @pl.when((step >= 2) & (step < n_tiles + 2))
    def _():
        t = step - 2
        copy2q(t).wait()
        s3[t] = silu(s2q[t].astype(jnp.float32) + r2q[t].astype(jnp.float32)).astype(jnp.bfloat16)
        copy3(t).start()
        copy2k(t).wait()
        own = silu(mine[t, x, :, tile:].astype(jnp.float32) + r2k[t].astype(jnp.float32))
        own = own.astype(jnp.bfloat16)
        kv[t] = own[:, :2 * tile]
        gate_ref[:, columns(t, tile)] = own[:, 2 * tile:]

    @pl.when((step >= 1) & (step < n_tiles + 1))
    def _():
        t = step - 1
        copy1(t).wait()
        for xx in range(2):
            both = mine[t, xx, :, :tile].astype(jnp.float32) + r1[t, xx, :, :tile].astype(jnp.float32)
            s2q[t, xx] = both.astype(jnp.bfloat16)
        copy2q(t).start()
        both = mine[t, 1 - x, :, tile:].astype(jnp.float32) + r1[t, 1 - x, :, tile:].astype(jnp.float32)
        s2k[t] = both.astype(jnp.bfloat16)
        copy2k(t).start()
        both = mine[t, x, :, tile:].astype(jnp.float32) + r1[t, x, :, tile:].astype(jnp.float32)
        mine[t, x, :, tile:] = both.astype(jnp.bfloat16)

    @pl.when((step >= 3) & (step < n_tiles + 3))
    def _():
        t = step - 3
        copy3(t).wait()
        for half in (1, 0):
            src = s3 if half == 0 else r3
            for h in range(tile // DH):
                cols = slice(h * DH, (h + 1) * DH)
                q = src[t, :, :, cols].reshape(2 * rows, DH)
                scores = lax.dot_general(
                    q, k_ref[:, columns(t, DH, h * DH)], (((1,), (1,)), ((), ())),
                    preferred_element_type=jnp.float32,
                )
                weights = (silu(scores * DH ** (-0.5)) * mask[half]).astype(jnp.bfloat16)
                out = jnp.dot(
                    weights, v_ref[:, columns(t, DH, h * DH)], preferred_element_type=jnp.float32
                ).reshape(2, rows, DH)
                if half == 0:
                    part[t, :, :, cols] = out
                else:
                    s4[t, :, :, cols] = out.astype(jnp.bfloat16)
            if half == 1:
                copy4(t).start()

    @pl.when(step < n_tiles)
    def _():
        t = step
        chunk = min(512, depth)
        for d in range(depth // chunk):
            block = w_ref[d * chunk:(d + 1) * chunk]
            flat = jnp.concatenate([block[:, j, :] for j in range(4)], axis=1)
            term = jnp.dot(
                tok_ref[:, d * chunk:(d + 1) * chunk], flat, preferred_element_type=jnp.float32
            )
            if d == 0:
                acc[...] = term
            else:
                acc[...] += term
        for xx in range(2):
            s1[t, xx] = acc[quarter(xx, 1 - c), :].astype(jnp.bfloat16)
        copy1(t).start()
        for xx in range(2):
            mine[t, xx] = acc[quarter(xx, c), :].astype(jnp.bfloat16)


def fused_history(tokens, w_qkvu, k_cache, v_cache, vis_start, vis_end):
    cand, depth = tokens.shape
    width = w_qkvu.shape[2]
    events = k_cache.shape[0]
    n_tiles = width // TILE
    rows = cand // 4
    lo = jnp.broadcast_to(vis_start[:, None], (cand, 128))
    hi = jnp.broadcast_to(vis_end[:, None], (cand, 128))

    def whole(shape):
        return pl.BlockSpec(shape, lambda i: (0, 0), pipeline_mode=pl.Buffered(1))

    def half(extra, cols):
        return pltpu.VMEM((n_tiles,) + extra + (rows, cols), jnp.bfloat16)

    return pl.pallas_call(
        functools.partial(history_kernel, n_tiles),
        grid=(n_tiles + 5,),
        in_specs=[
            whole((cand, depth)),
            pl.BlockSpec((depth, 4, TILE), lambda i: (0, 0, jnp.minimum(i, n_tiles - 1))),
            whole((events, width)),
            whole((events, width)),
            whole((cand, 128)),
            whole((cand, 128)),
        ],
        out_specs=[whole((rows, width)), whole((rows, width))],
        out_shape=[
            jax.ShapeDtypeStruct((rows, width), jnp.float32),
            jax.ShapeDtypeStruct((rows, width), jnp.bfloat16),
        ],
        scratch_shapes=[
            pltpu.VMEM((cand, 4 * TILE), jnp.float32),
            pltpu.VMEM((2, 2 * rows, events), jnp.float32),
            half((2,), 4 * TILE),
            half((2,), 4 * TILE), half((2,), 4 * TILE),
            half((2,), TILE), half((2,), TILE),
            half((), 3 * TILE), half((), 3 * TILE),
            half((2,), TILE), half((2,), TILE),
            half((), 2 * TILE),
            half((2,), TILE), half((2,), TILE),
            pltpu.VMEM((n_tiles, 2, rows, TILE), jnp.float32),
            half((), TILE), half((), TILE),
            pltpu.SemaphoreType.DMA((6, n_tiles)),
            pltpu.SemaphoreType.DMA((6, n_tiles)),
        ],
        compiler_params=pltpu.CompilerParams(
            vmem_limit_bytes=62 << 20, collective_id=0, has_side_effects=True
        ),
        name="history",
    )(tokens, w_qkvu, k_cache, v_cache, lo, hi)


def output_kernel(
    att_ref, gate_ref, w_hbm, tok_hbm, out_ref,
    w_out, res, stat, got, units, own, near, far, relay, passed,
    load_sem, st_s, st_r, g_s, g_r, u_s, near_r, far_r, relay_r,
):
    mesh_id = pl.DeviceIdType.MESH
    me = lax.axis_index("hist")
    z = lax.axis_index("head")
    x = me // 2
    c = me % 2
    partner = 2 * x + (1 - c)
    across = 2 * (1 - x) + c
    peer = 2 * (z // 2) + 1 - z % 2
    inner = (z // 2) != (z % 2)
    rows, width = att_ref.shape
    piece = out_ref.shape[1] // 2
    quarters = (me, partner, across, 2 * (1 - x) + (1 - c))

    load_w = pltpu.make_async_copy(w_hbm, w_out, load_sem.at[0])
    load_w.start()
    load_t = pltpu.make_async_copy(
        tok_hbm.at[pl.ds(pl.multiple_of(z * rows, rows), rows), :], res, load_sem.at[1]
    )
    load_t.start()

    barrier = pltpu.get_barrier_semaphore()
    for other in (partner, across):
        pl.semaphore_signal(barrier, inc=1, device_id={"hist": other}, device_id_type=mesh_id)
    for k in range(1, 4):
        pl.semaphore_signal(
            barrier, inc=1, device_id={"head": (z + k) % 4}, device_id_type=mesh_id
        )
    pl.semaphore_wait(barrier, 5)

    att = att_ref[...]
    local_mean = jnp.sum(att, axis=1, keepdims=True) / width
    off = att - local_mean
    local_sq = jnp.sum(off * off, axis=1, keepdims=True)
    lane = lax.broadcasted_iota(jnp.int32, (rows, 128), 1)
    stat[0] = jnp.where(lane < 64, local_mean, local_sq)
    stat_copies = []
    for k in range(1, 4):
        cp = pltpu.make_async_remote_copy(
            src_ref=stat.at[0], dst_ref=stat.at[k], send_sem=st_s.at[k - 1],
            recv_sem=st_r.at[k - 1], device_id={"head": (z + k) % 4}, device_id_type=mesh_id,
        )
        cp.start()
        stat_copies.append(cp)
    for cp in stat_copies:
        cp.wait()
    means = [stat[k, :, 0:1] for k in range(4)]
    mean = (means[0] + means[1] + means[2] + means[3]) / 4
    spread = jnp.zeros_like(mean)
    for k in range(4):
        shift = means[k] - mean
        spread = spread + stat[k, :, 127:128] + width * shift * shift
    inv = lax.rsqrt(spread / (4 * width) + epsilon)
    got[0] = ((att_ref[...] - mean) * inv * gate_ref[...].astype(jnp.float32)).astype(jnp.bfloat16)

    def gather(k, src, dst, target):
        return pltpu.make_async_remote_copy(
            src_ref=got.at[src], dst_ref=got.at[dst], send_sem=g_s.at[k], recv_sem=g_r.at[k],
            device_id={"hist": target}, device_id_type=mesh_id,
        )

    to_across = gather(1, 0, 2, across)
    to_across.start()
    to_partner = gather(0, 0, 1, partner)
    to_partner.start()
    pass_on = gather(2, 2, 3, partner)

    def unit_copy(i, p, src, dst, recv_sem, target):
        return pltpu.make_async_remote_copy(
            src_ref=src, dst_ref=dst, send_sem=u_s.at[i, p], recv_sem=recv_sem,
            device_id={"head": target}, device_id_type=mesh_id,
        )

    def is_far(i):
        return (quarters[i] // 2) != (z // 2)

    def near_copy(i, p):
        return unit_copy(i, p, units.at[i, p], near.at[p], near_r.at[p], peer)

    def relay_copy(i, p):
        slot = quarters[i] % 2
        return unit_copy(i, p, units.at[i, p], relay.at[slot, p], relay_r.at[slot, p], peer)

    def far_copy(i, p):
        r = quarters[i]
        return unit_copy(i, p, passed.at[r % 2, p], far.at[p], far_r.at[p], r)

    def multiply(pair, p):
        both = got[2 * pair:2 * pair + 2].reshape(2 * rows, width)
        acc = jnp.dot(
            both, w_out[:, p * piece:(p + 1) * piece], preferred_element_type=jnp.float32
        )
        for k in range(2):
            i = 2 * pair + k
            term = acc[k * rows:(k + 1) * rows]
            units[i, p] = term.astype(jnp.bfloat16)

            @pl.when(quarters[i] == z)
            def _():
                own[p] = term

            @pl.when(quarters[i] == peer)
            def _():
                near_copy(i, p).start()

            @pl.when(is_far(i) & jnp.logical_not(inner))
            def _():
                relay_copy(i, p).start()

    def forward(pair):
        for p in range(2):
            for k in range(2):
                i = 2 * pair + k

                @pl.when(is_far(i) & inner)
                def _():
                    relay_copy(i, p).wait_recv()
                    slot = quarters[i] % 2
                    total = units[i, p].astype(jnp.float32) + relay[slot, p].astype(jnp.float32)
                    passed[slot, p] = total.astype(jnp.bfloat16)
                    far_copy(i, p).start()

    load_w.wait()
    to_partner.wait()
    multiply(0, 0)
    multiply(0, 1)
    to_across.wait()
    pass_on.start()
    pass_on.wait()
    multiply(1, 0)
    forward(0)
    multiply(1, 1)
    forward(1)
    load_t.wait()
    for p in range(2):
        near_copy(0, p).wait_recv()
        far_copy(0, p).wait_recv()
        total = own[p] + near[p].astype(jnp.float32) + far[p].astype(jnp.float32)
        cols = slice(p * piece, (p + 1) * piece)
        out_ref[:, cols] = (res[:, cols].astype(jnp.float32) + total).astype(jnp.bfloat16)
    for i in range(4):
        for p in range(2):
            @pl.when(quarters[i] != z)
            def _():
                near_copy(i, p).wait_send()


def fused_output(attended, gate, w_out, tokens):
    rows, width = attended.shape
    cols = w_out.shape[1]
    piece = cols // 2
    vmem = pl.BlockSpec(memory_space=pltpu.VMEM)
    anywhere = pl.BlockSpec(memory_space=pl.ANY)
    dma = pltpu.SemaphoreType.DMA

    def slots(*lead):
        return pltpu.VMEM(lead + (rows, piece), jnp.bfloat16)

    return pl.pallas_call(
        output_kernel,
        in_specs=[vmem, vmem, anywhere, anywhere],
        out_specs=vmem,
        out_shape=jax.ShapeDtypeStruct((rows, cols), jnp.bfloat16),
        scratch_shapes=[
            pltpu.VMEM((width, cols), jnp.bfloat16),
            pltpu.VMEM((rows, cols), jnp.bfloat16),
            pltpu.VMEM((4, rows, 128), jnp.float32),
            pltpu.VMEM((4, rows, width), jnp.bfloat16),
            slots(4, 2),
            pltpu.VMEM((2, rows, piece), jnp.float32),
            slots(2), slots(2), slots(2, 2), slots(2, 2),
            dma((2,)), dma((3,)), dma((3,)), dma((3,)), dma((3,)),
            dma((4, 2)), dma((2,)), dma((2,)), dma((2, 2)),
        ],
        compiler_params=pltpu.CompilerParams(
            vmem_limit_bytes=60 << 20, collective_id=1, has_side_effects=True
        ),
        name="output",
    )(attended, gate, w_out, tokens)


def local_fused(tokens, w_qkvu, k_cache, v_cache, w_out, vis_start, vis_end):
    attended, gate = fused_history(tokens, w_qkvu, k_cache, v_cache, vis_start, vis_end)
    return fused_output(attended, gate, w_out, tokens)


def solution(mesh):
    in_specs = (
        P("groups", "hist"),
        P("hist", None, "head"),
        P(("groups", "hist"), "head"),
        P(("groups", "hist"), "head"),
        P("head", "hist"),
        P("groups"),
        P("groups"),
    )
    out_specs = P(("groups", "head"), "hist")
    body = local_fused if mesh.shape["hist"] == 4 and mesh.shape["head"] == 4 else local
    return jax.shard_map(body, mesh=mesh, in_specs=in_specs, out_specs=out_specs, check_vma=False)
```
